1024 devices in a mesh: layer: 2 (over x_hi), row: 64 (over z, x_lo, core), col: 8 (over y).
Axes of the slice: x: 4 (x_hi: 2, x_lo: 2; x = x_hi * 2 + x_lo), y: 8, z: 16, core: 2. Of those that a mesh axis runs over, the one named last changes fastest.
Arguments:
- slab_tiles: bfloat16 [128, 256, 2, 8, 128], P(None, 'row', 'layer'), may hold values from -0.0390625 to 0.0390625
- x_tiles: bfloat16 [1024, 8, 2, 128, 128], P(('layer', 'row', 'col')), may hold values from -6 to 6
- x_cols: int32 [1024, 8, 2], P(('layer', 'row', 'col')), may hold values from 0 to 1023, as said below
- x2_tiles: bfloat16 [1024, 8, 2, 128, 128], P(('layer', 'row', 'col')), may hold values from -6 to 6
- x2_cols: int32 [1024, 8, 2], P(('layer', 'row', 'col')), may hold values from 0 to 1023, as said below
- requests: int32 [2, 64, 8], P('layer'), may hold values from 0 to 1023, as said below
- out_cols: int32 [64, 8, 4], P('row', 'col'), may hold values from 0 to 1023, as said below
Outputs:
- purified: bfloat16 [128, 256, 8, 4, 128], P('layer', 'row', 'col')
The draws below stay inside these ranges and needn't reach their ends.
Inputs may be any that keep to these rules, and one draw needn't show every extreme that they name: Block row k is held by the device at index k of layer, row and col taken together. requests[l, r, q] is a block row held by layer l at row index (r + q * 8) % 64; every block row held by layer l is named exactly once in requests[l]. out_cols[r, c] holds 4 distinct block columns j, each with j % 8 == c. x_cols[k, c] holds 2 distinct block columns taken from out_cols[r, c], where r is the group whose requests name k. x2_cols[k, c] holds 2 distinct block columns taken from out_cols[r, c], where r is the group whose requests name k.
All inputs are finite; a program needn't handle non-finite values.
Results may differ from the reference program's by a relative error of at most 0.001.
Values may be sent and summed in bfloat16 or wider, within the bound.
A program may use at most 32 MiB of HBM per device.

```python
import jax
import jax.numpy as jnp
from jax import lax

BS = 128
SR = 4
NZC = 2
NOUT = 4
NB = 1024
REQ = 8
SLAB = 256
N_LAYER = 2
N_ROW = 64
N_COL = 8


def build_requests(key):
    order_keys = jax.random.split(jax.random.fold_in(key, 202), N_LAYER * N_ROW)

    def col_order(sub_key):
        return jax.random.permutation(sub_key, N_COL)
    orders = jax.vmap(col_order)(order_keys).reshape(N_LAYER, N_ROW, N_COL)
    layer_ids = jnp.arange(N_LAYER, dtype=jnp.int32)[:, None, None]
    group_ids = jnp.arange(N_ROW, dtype=jnp.int32)[None, :, None]
    slot_ids = jnp.arange(N_COL, dtype=jnp.int32)[None, None, :]
    owner_rows = (group_ids + slot_ids * (N_ROW // N_COL)) % N_ROW
    owner_cols = orders[layer_ids, owner_rows, slot_ids]
    return ((layer_ids * N_ROW + owner_rows) * N_COL + owner_cols).astype(jnp.int32)


def build_out_cols(key):
    pair_keys = jax.random.split(jax.random.fold_in(key, 303), N_ROW * N_COL)

    def pick_cols(sub_key):
        return jax.random.permutation(sub_key, N_LAYER * N_ROW)[:NOUT]
    chosen = jax.vmap(pick_cols)(pair_keys).reshape(N_ROW, N_COL, NOUT)
    return (chosen * N_COL + jnp.arange(N_COL, dtype=jnp.int32)[None, :, None]).astype(jnp.int32)


def build_cols(key, salt_value):
    requests = build_requests(key)
    targets = build_out_cols(key)
    group_ids = jnp.broadcast_to(jnp.arange(N_ROW, dtype=jnp.int32)[None, :, None], requests.shape)
    group_of = jnp.zeros((NB,), jnp.int32).at[requests.reshape(-1)].set(group_ids.reshape(-1))
    slot_keys = jax.random.split(jax.random.fold_in(key, salt_value), NB * N_COL)

    def pick_slots(sub_key):
        return jax.random.permutation(sub_key, NOUT)[:NZC]
    slot_picks = jax.vmap(pick_slots)(slot_keys).reshape(NB, N_COL, NZC)
    column_ids = jnp.arange(N_COL, dtype=jnp.int32)[None, :, None]
    return targets[group_of[:, None, None], column_ids, slot_picks].astype(jnp.int32)


def draw_requests(key, part):
    return build_requests(key)


def draw_out_cols(key, part):
    return build_out_cols(key)


def draw_x_cols(key, part):
    return build_cols(key, 404)


def draw_x2_cols(key, part):
    return build_cols(key, 505)


def shard_levels(own_key, dims, shards, least, top_value):
    level = 1.0
    for axis_at, shards_of in shards:
        draws = jax.random.uniform(jax.random.fold_in(jax.random.fold_in(own_key, 6), axis_at), (shards_of,), jnp.float32, least / len(shards), top_value / len(shards))
        level = level * jnp.repeat(jnp.exp(draws), dims[axis_at] // shards_of).reshape((-1,) + (1,) * (len(dims) - 1 - axis_at))
    return level


def centred(rng, shape, spread, limit, cuts=(), held_as=jnp.bfloat16):
    gain = shard_levels(rng, shape, cuts, -0.22, 0.18) if cuts else 1.0
    values = jax.random.normal(rng, shape, jnp.float32) * spread * gain
    return jnp.minimum(jnp.maximum(values, -limit), limit).astype(held_as)


def setup_inputs(seed: int = 0) -> dict:
    arg_keys = jax.random.split(jax.random.key(seed), 8)
    return {
        "slab_tiles": centred(arg_keys[0], (BS, SLAB, N_LAYER, REQ, BS), (25 * N_LAYER * N_COL * BS * NZC // NOUT) ** -0.5, 0.0390625, ((1, 64), (2, 2))),
        "x_tiles": centred(arg_keys[1], (NB, N_COL, NZC, BS, BS), 1.0, 6.0, ((0, 1024),)),
        "x_cols": draw_x_cols(jax.random.fold_in(arg_keys[7], 71), 0),
        "x2_tiles": centred(arg_keys[3], (NB, N_COL, NZC, BS, BS), 1.0, 6.0, ((0, 1024),)),
        "x2_cols": draw_x2_cols(jax.random.fold_in(arg_keys[7], 71), 0),
        "requests": draw_requests(jax.random.fold_in(arg_keys[7], 71), 0),
        "out_cols": draw_out_cols(jax.random.fold_in(arg_keys[7], 71), 0),
    }


def choose_tiles(tile_set, col_ids, picked, targets):
    gathered = tile_set[picked].astype(jnp.float32)
    listed = col_ids[picked]
    matches = (listed[:, :, :, None] == targets[None, :, None, :]).astype(jnp.float32)
    chosen = jnp.einsum('kcus,kcubd->kbcsd', matches, gathered)
    return chosen.astype(jnp.bfloat16).reshape(picked.shape[0] * BS, N_COL * NOUT * BS)


def reference(slab_tiles, x_tiles, x_cols, x2_tiles, x2_cols, requests, out_cols):
    def one_group(grid_row):
        picked = lax.dynamic_index_in_dim(requests, grid_row, 1, keepdims=False).reshape(-1).astype(jnp.int32)
        targets = lax.dynamic_index_in_dim(out_cols, grid_row, 0, keepdims=False)
        a_block = lax.dynamic_slice_in_dim(slab_tiles, (grid_row * SR).astype(jnp.int32), SR, 1)
        a_block = a_block.reshape(BS * SR, N_LAYER * REQ * BS)
        first_term = jnp.dot(a_block, choose_tiles(x_tiles, x_cols, picked, targets), preferred_element_type=jnp.float32)
        second_term = jnp.dot(a_block, choose_tiles(x2_tiles, x2_cols, picked, targets), preferred_element_type=jnp.float32)
        combined = (4.0 * first_term - 3.0 * second_term).astype(jnp.bfloat16)
        return combined.reshape(BS, SR, N_COL, NOUT, BS)

    blocks = lax.map(one_group, jnp.arange(N_ROW, dtype=jnp.int32))
    return jnp.transpose(blocks, (1, 0, 2, 3, 4, 5)).reshape(BS, SLAB, N_COL, NOUT, BS)
```

```python
import functools

import jax
import jax.numpy as jnp
from jax import lax
from jax.experimental import pallas as pl
from jax.experimental.pallas import tpu as pltpu
from jax.sharding import PartitionSpec as P

MESH = pl.DeviceIdType.MESH
BS = 128
NCH = 4
QW = BS // NCH
NT = 4
EXTRA = 16


def one_hot(cond):
    return jnp.where(cond, 1.0, 0.0).astype(jnp.bfloat16)


def iota(shape, dim):
    return lax.broadcasted_iota(jnp.int32, shape, dim)


def kernel(
    sizes, x_hbm, x2_hbm, a_hbm, xc, x2c, req, oc, out_ref, xv, a_raw, a2, pt, w, rs_send, rs_recv,
    own, *rest
):
    n_row, n_col, n_req = sizes
    y_send, y_recv, z_send, z_recv = (rest[i * NCH : (i + 1) * NCH] for i in range(4))
    load_sem, y_ss, y_rs, z_ss, z_rs, r_ss, r_rs = rest[4 * NCH :]
    layer, row, col = (lax.axis_index(a) for a in ("layer", "row", "col"))
    stride = n_row // n_col
    half = own.shape[1]

    loads = [
        pltpu.make_async_copy(x_hbm, xv.at[0], load_sem.at[0]),
        pltpu.make_async_copy(x2_hbm, xv.at[1], load_sem.at[1]),
        pltpu.make_async_copy(a_hbm, a_raw, load_sem.at[2]),
    ]
    for load in loads:
        load.start()

    barrier = pltpu.get_barrier_semaphore()
    peers = [(layer, row, lax.rem(col + d, n_col)) for d in range(1, n_col)]
    peers += [(layer, lax.rem(row + stride * q, n_row), col) for q in range(1, n_req)]
    peers += [(1 - layer, row, col)]
    for peer in peers:
        pl.semaphore_signal(barrier, inc=1, device_id=peer, device_id_type=MESH)

    def rows_sent(j):
        return BS + EXTRA if j == 0 else BS

    def y_copy(j, d):
        n = rows_sent(j)
        to = lax.rem(col + d, n_col)
        return pltpu.make_async_remote_copy(
            src_ref=y_send[j].at[to, pl.ds(0, n)],
            dst_ref=y_recv[j].at[col, pl.ds(0, n)],
            send_sem=y_ss.at[j, d],
            recv_sem=y_rs.at[j, d],
            device_id=(layer, row, to),
            device_id_type=MESH,
        )

    def z_copy(j, q):
        n = rows_sent(j)
        return pltpu.make_async_remote_copy(
            src_ref=z_send[j].at[q, pl.ds(0, n)],
            dst_ref=z_recv[j].at[q, pl.ds(0, n)],
            send_sem=z_ss.at[j, q],
            recv_sem=z_rs.at[j, q],
            device_id=(layer, lax.rem(row - stride * q + n_row, n_row), col),
            device_id_type=MESH,
        )

    def r_copy(j):
        return pltpu.make_async_remote_copy(
            src_ref=rs_send.at[j],
            dst_ref=rs_recv.at[j],
            send_sem=r_ss.at[j],
            recv_sem=r_rs.at[j],
            device_id=(1 - layer, row, col),
            device_id_type=MESH,
        )

    y_order = sorted(range(1, n_col), key=lambda d: abs(2 * d - n_col))
    z_order = sorted(range(1, n_req), key=lambda q: abs(2 * q - n_req))

    loads[0].wait()
    loads[1].wait()
    lane = iota((EXTRA, BS), 1)

    for j in range(NCH):
        src, dst = iota((NT * BS, BS), 0), iota((NT * BS, BS), 1)
        take = one_hot(
            (src // BS == dst // QW) & (lax.rem(src, BS) == lax.rem(dst, QW) + j * QW)
        )

        def build(c, carry, j=j, take=take):
            tiles = jnp.concatenate([xv[0, c, 0], xv[0, c, 1], xv[1, c, 0], xv[1, c, 1]], axis=1)
            chunk = jnp.dot(tiles, take, preferred_element_type=jnp.float32)
            y_send[j][c, 0:BS] = chunk.astype(jnp.bfloat16)
            if j == 0:
                first = jnp.where(lane < QW, xc[0, 0, c], xc[0, 1, c])
                second = jnp.where(lane < 3 * QW, x2c[0, 0, c], x2c[0, 1, c])
                ids = jnp.where(lane < 2 * QW, first, second) >> 3
                y_send[0][c, BS : BS + EXTRA] = ids.astype(jnp.float32).astype(jnp.bfloat16)
            return carry

        lax.fori_loop(0, n_col, build, 0, unroll=True)
        if j == 0:
            pl.semaphore_wait(barrier, len(peers))
        for d in y_order:
            y_copy(j, d).start()
        y_recv[j][col] = y_send[j][col]

    owners = []
    for q in range(n_req):
        reader = lax.rem(row - stride * q + n_row, n_row)
        owners.append(lax.rem(req[0, q, reader], n_col))

    def forward(j):
        for d in y_order:
            y_copy(j, d).wait_recv()
        n = rows_sent(j)
        for q in z_order:
            z_send[j][q, 0:n] = y_recv[j][owners[q], 0:n]
            z_copy(j, q).start()
        z_recv[j][0, 0:n] = y_recv[j][owners[0], 0:n]

    forward(0)

    loads[2].wait()
    group = BS // n_req
    to_row, from_row = iota((BS, BS), 0), iota((BS, BS), 1)
    swap = one_hot(
        (to_row // group == lax.rem(from_row, n_req)) & (lax.rem(to_row, group) == from_row // n_req)
    )

    def regroup(i, carry):
        block = a_raw[pl.ds(pl.multiple_of(i * BS, BS), BS), :]
        moved = jnp.dot(swap, block, preferred_element_type=jnp.float32).astype(jnp.bfloat16)
        for q in range(n_req):
            a2[pl.ds(pl.multiple_of(i * group, group), group), q * BS : (q + 1) * BS] = moved[
                q * group : (q + 1) * group
            ]
        return carry

    lax.fori_loop(0, a_raw.shape[0] // BS, regroup, 0, unroll=4)

    for j in range(1, NCH):
        forward(j)

    target_row = lax.rem(iota((2 * BS, BS), 0), BS) // QW
    target = jnp.where(
        target_row < 2,
        jnp.where(target_row < 1, oc[0, 0, 0], oc[0, 0, 1]),
        jnp.where(target_row < 3, oc[0, 0, 2], oc[0, 0, 3]),
    )
    target = (target >> 3).astype(jnp.float32)
    same_column = lax.rem(iota((2 * BS, BS), 0), QW) == lax.rem(iota((2 * BS, BS), 1), QW)
    same_set = iota((2 * BS, BS), 0) // BS == iota((2 * BS, BS), 1) // (2 * QW)

    def terms(j, start):
        part = jnp.dot(a2[pl.ds(start, half), :], w[...], preferred_element_type=jnp.float32)
        return 4.0 * part[:, :BS] - 3.0 * part[:, BS:]

    own_start = pl.multiple_of(layer * half, half)
    other_start = pl.multiple_of((1 - layer) * half, half)
    for j in range(NCH):
        for q in z_order:
            z_copy(j, q).wait_recv()
        for q in range(n_req):
            if j == 0:
                ids = z_recv[0][q, BS : BS + EXTRA].astype(jnp.float32)[0:1]
                pt[q] = one_hot((ids == target) & same_column & same_set)
            placed = lax.dot_general(
                z_recv[j][q, 0:BS],
                pt[q],
                (((1,), (1,)), ((), ())),
                preferred_element_type=jnp.float32,
            )
            w[q * BS : (q + 1) * BS, :] = placed.astype(jnp.bfloat16)
        rs_send[j] = terms(j, other_start)
        r_copy(j).start()
        own[j] = terms(j, own_start)

    total = jnp.zeros((half, NT * BS), jnp.float32)
    for j in range(NCH):
        r_copy(j).wait_recv()
        summed = (own[j] + rs_recv[j]).astype(jnp.bfloat16)
        src, dst = iota((BS, NT * BS), 0), iota((BS, NT * BS), 1)
        put = one_hot((dst // BS == src // QW) & (lax.rem(dst, BS) == lax.rem(src, QW) + j * QW))
        total = total + jnp.dot(summed, put, preferred_element_type=jnp.float32)
    out_ref[...] = total.astype(jnp.bfloat16)

    for j in range(NCH):
        for d in y_order:
            y_copy(j, d).wait_send()
        for q in z_order:
            z_copy(j, q).wait_send()
        r_copy(j).wait_send()


def body(slab_tiles, x_tiles, x_cols, x2_tiles, x2_cols, requests, out_cols):
    n_row, n_col = lax.axis_size("row"), lax.axis_size("col")
    bs, sr, _, n_req, _ = slab_tiles.shape
    n_out = out_cols.shape[2]
    rows = bs * sr
    half = rows // 2
    vmem, smem = pl.BlockSpec(memory_space=pltpu.VMEM), pl.BlockSpec(memory_space=pltpu.SMEM)
    anywhere = pl.BlockSpec(memory_space=pl.ANY)
    bf16, f32 = jnp.bfloat16, jnp.float32
    out = pl.pallas_call(
        functools.partial(kernel, (n_row, n_col, n_req)),
        name="purify",
        out_shape=jax.ShapeDtypeStruct((half, n_out * bs), bf16),
        in_specs=[anywhere, anywhere, anywhere, smem, smem, smem, smem],
        out_specs=vmem,
        scratch_shapes=[
            pltpu.VMEM((2, n_col, 2, bs, bs), bf16),
            pltpu.VMEM((rows * n_req, bs), bf16),
            pltpu.VMEM((rows, n_req * bs), bf16),
            pltpu.VMEM((n_req, 2 * bs, bs), bf16),
            pltpu.VMEM((n_req * bs, 2 * bs), bf16),
            pltpu.VMEM((NCH, half, bs), f32),
            pltpu.VMEM((NCH, half, bs), f32),
            pltpu.VMEM((NCH, half, bs), f32),
        ]
        + [pltpu.VMEM((n_col, bs + EXTRA, bs), bf16)] * (2 * NCH)
        + [pltpu.VMEM((n_req, bs + EXTRA, bs), bf16)] * (2 * NCH)
        + [
            pltpu.SemaphoreType.DMA((3,)),
            pltpu.SemaphoreType.DMA((NCH, n_col)),
            pltpu.SemaphoreType.DMA((NCH, n_col)),
            pltpu.SemaphoreType.DMA((NCH, n_req)),
            pltpu.SemaphoreType.DMA((NCH, n_req)),
            pltpu.SemaphoreType.DMA((NCH,)),
            pltpu.SemaphoreType.DMA((NCH,)),
        ],
        compiler_params=pltpu.CompilerParams(collective_id=0, has_side_effects=True),
    )(
        x_tiles.reshape(x_tiles.shape[1:]),
        x2_tiles.reshape(x2_tiles.shape[1:]),
        slab_tiles.reshape(rows * n_req, bs),
        jnp.swapaxes(x_cols, 1, 2),
        jnp.swapaxes(x2_cols, 1, 2),
        jnp.swapaxes(requests, 1, 2),
        out_cols,
    )
    return out.reshape(bs // 2, sr, 1, n_out, bs)


def solution(mesh):
    placed = (
        P(None, "row", "layer", None, None),
        P(("layer", "row", "col"), None, None, None, None),
        P(("layer", "row", "col"), None, None),
        P(("layer", "row", "col"), None, None, None, None),
        P(("layer", "row", "col"), None, None),
        P("layer", None, None),
        P("row", "col", None),
    )
    return jax.shard_map(
        body,
        mesh=mesh,
        in_specs=placed,
        out_specs=P("layer", "row", "col", None, None),
        check_vma=False,
    )
```

```python
import functools

import jax
import jax.numpy as jnp
from jax import lax
from jax.experimental import pallas as pl
from jax.experimental.pallas import tpu as pltpu
from jax.sharding import PartitionSpec as P

MESH = pl.DeviceIdType.MESH
BS = 128
NCH = 4
QW = BS // NCH
NT = 4
EXTRA = 16
PIECES = (
    (0, 0, 16), (0, 16, 32), (0, 48, 64), (0, 112, 16), (1, 0, 128), (2, 0, 128), (3, 0, 128)
)


def one_hot(cond):
    return jnp.where(cond, 1.0, 0.0).astype(jnp.bfloat16)


def iota(shape, dim):
    return lax.broadcasted_iota(jnp.int32, shape, dim)


IDS = max(p for p in range(len(PIECES)) if PIECES[p][0] == 0)


def piece_rows(p):
    return PIECES[p][2] + (EXTRA if p == IDS else 0)


def kernel(
    sizes, x_hbm, x2_hbm, a_hbm, xc_hbm, x2c_hbm, req_hbm, oc_hbm, out_ref, xc, x2c, req, oc, xv, a_raw, a2, pt, w, rs_send, rs_recv,
    own, total, *rest
):
    n_row, n_col, n_req = sizes
    n_p = len(PIECES)
    y_send, y_recv, z_send, z_recv = (rest[i * n_p : (i + 1) * n_p] for i in range(4))
    load_sem, y_ss, y_rs, z_ss, z_rs, r_ss, r_rs, y_hello, z_hello = rest[4 * n_p :]
    layer, row, col = (lax.axis_index(a) for a in ("layer", "row", "col"))
    stride = n_row // n_col
    place = row // stride
    half = own.shape[1]

    loads = [
        pltpu.make_async_copy(x_hbm, xv.at[0], load_sem.at[0]),
        pltpu.make_async_copy(x2_hbm, xv.at[1], load_sem.at[1]),
        pltpu.make_async_copy(a_hbm, a_raw, load_sem.at[2]),
        pltpu.make_async_copy(req_hbm, req, load_sem.at[3]),
        pltpu.make_async_copy(xc_hbm, xc, load_sem.at[4]),
        pltpu.make_async_copy(x2c_hbm, x2c, load_sem.at[5]),
        pltpu.make_async_copy(oc_hbm, oc, load_sem.at[6]),
    ]
    def y_device(d):
        return (layer, row, lax.rem(col + d, n_col))

    def z_device(q):
        return (layer, lax.rem(row - stride * q + n_row, n_row), col)

    def y_lower(d):
        return col + d >= n_col

    def z_lower(q):
        return q <= place

    barrier = pltpu.get_barrier_semaphore()

    def signal(sem, device):
        pl.semaphore_signal(sem, inc=1, device_id=device, device_id_type=MESH)

    signal(barrier, (1 - layer, row, col))
    for d in range(1, n_col):
        pl.when(jnp.logical_not(y_lower(d)))(functools.partial(signal, barrier, y_device(d)))
    for q in range(1, n_req):
        pl.when(jnp.logical_not(z_lower(q)))(functools.partial(signal, barrier, z_device(q)))

    for load in loads:
        load.start()

    pl.semaphore_wait(barrier, 1 + col + place)
    for q in range(1, n_req):
        pl.when(z_lower(q))(functools.partial(signal, z_hello.at[n_req - q], z_device(q)))
    for d in range(1, n_col):
        pl.when(y_lower(d))(functools.partial(signal, y_hello.at[n_col - d], y_device(d)))

    def y_copy(p, d):
        return pltpu.make_async_remote_copy(
            src_ref=y_send[p].at[lax.rem(col + d, n_col)],
            dst_ref=y_recv[p].at[col],
            send_sem=y_ss.at[p, d],
            recv_sem=y_rs.at[p, d],
            device_id=y_device(d),
            device_id_type=MESH,
        )

    def z_copy(p, q):
        return pltpu.make_async_remote_copy(
            src_ref=z_send[p].at[q],
            dst_ref=z_recv[p].at[q],
            send_sem=z_ss.at[p, q],
            recv_sem=z_rs.at[p, q],
            device_id=z_device(q),
            device_id_type=MESH,
        )

    def r_copy(j):
        return pltpu.make_async_remote_copy(
            src_ref=rs_send.at[j],
            dst_ref=rs_recv.at[j],
            send_sem=r_ss.at[j],
            recv_sem=r_rs.at[j],
            device_id=(1 - layer, row, col),
            device_id_type=MESH,
        )

    y_order = sorted(range(1, n_col), key=lambda d: abs(2 * d - n_col))
    z_order = sorted(range(1, n_req), key=lambda q: abs(2 * q - n_req))

    def heard(sem, *copies):
        pl.semaphore_wait(sem, 1)
        for copy in copies:
            copy.start()

    def build(p):
        j, at, n = PIECES[p]
        src, dst = iota((NT * BS, BS), 0), iota((NT * BS, BS), 1)
        take = one_hot(
            (src // BS == dst // QW) & (lax.rem(src, BS) == lax.rem(dst, QW) + j * QW)
        )
        group = n_col if n <= 32 else 1
        for c in range(0, n_col, group):
            tiles = [
                xv[i, c : c + group, u, at : at + n].reshape(group * n, BS)
                for i in range(2)
                for u in range(2)
            ]
            chunk = jnp.dot(
                jnp.concatenate(tiles, axis=1), take, preferred_element_type=jnp.float32
            )
            y_send[p][c : c + group, 0:n] = chunk.astype(jnp.bfloat16).reshape(group, n, BS)
        if p == IDS:
            lane = iota((EXTRA, BS), 1)
            for c in range(n_col):
                first = jnp.where(lane < QW, xc[0, 0, c], xc[0, 1, c])
                second = jnp.where(lane < 3 * QW, x2c[0, 0, c], x2c[0, 1, c])
                ids = jnp.where(lane < 2 * QW, first, second) >> 3
                y_send[p][c, n : n + EXTRA] = ids.astype(jnp.float32).astype(jnp.bfloat16)

    def send(p):
        for d in y_order:
            if p == 0:
                pl.when(y_lower(d))(y_copy(p, d).start)
            else:
                y_copy(p, d).start()
        if p == 0:
            for d in range(1, n_col):
                wait = functools.partial(heard, y_hello.at[d], y_copy(p, d))
                pl.when(jnp.logical_not(y_lower(d)))(wait)
        y_recv[p][col] = y_send[p][col]

    def forward(p):
        for d in y_order:
            y_copy(p, d).wait_recv()
        for q in z_order:
            z_send[p][q] = y_recv[p][owners[q]]
            if p <= 1:
                pl.when(z_lower(q))(z_copy(p, q).start)
            else:
                z_copy(p, q).start()
        z_recv[p][0] = y_recv[p][owners[0]]

    def upper(pieces, steps, wait):
        for k in steps:
            q = n_req - k
            copies = [z_copy(p, q) for p in pieces]

            def go(q=q, copies=copies):
                if wait:
                    heard(z_hello.at[q], *copies)
                else:
                    for copy in copies:
                        copy.start()

            pl.when(jnp.logical_not(z_lower(q)))(go)

    loads[0].wait()
    loads[1].wait()
    build(0)
    send(0)
    build(1)
    send(1)
    build(2)
    send(2)
    for load in loads[3:]:
        load.wait()
    owners = []
    for q in range(n_req):
        reader = lax.rem(row - stride * q + n_row, n_row)
        owners.append(lax.rem(req[0, q, reader], n_col))

    build(3)
    send(3)

    group = BS // n_req
    to_row, from_row = iota((BS, BS), 0), iota((BS, BS), 1)
    swap = one_hot(
        (to_row // group == lax.rem(from_row, n_req)) & (lax.rem(to_row, group) == from_row // n_req)
    )

    def regroup(i, carry):
        block = a_raw[pl.ds(pl.multiple_of(i * BS, BS), BS), :]
        moved = jnp.dot(swap, block, preferred_element_type=jnp.float32).astype(jnp.bfloat16)
        for q in range(n_req):
            a2[pl.ds(pl.multiple_of(i * group, group), group), q * BS : (q + 1) * BS] = moved[
                q * group : (q + 1) * group
            ]
        return carry

    forward(0)
    upper((0,), (1, 2), True)
    build(4)
    send(4)
    forward(1)
    upper((1,), (1, 2), False)
    upper((0, 1), (3, 4), True)
    loads[2].wait()
    lax.fori_loop(0, a_raw.shape[0] // BS, regroup, 0, unroll=4)
    upper((0, 1), range(5, n_req), True)
    forward(2)
    build(5)
    send(5)
    forward(3)
    build(6)
    send(6)
    for p in range(4, n_p):
        forward(p)

    target_row = lax.rem(iota((2 * BS, BS), 0), BS) // QW
    target = jnp.where(
        target_row < 2,
        jnp.where(target_row < 1, oc[0, 0, 0], oc[0, 0, 1]),
        jnp.where(target_row < 3, oc[0, 0, 2], oc[0, 0, 3]),
    )
    target = (target >> 3).astype(jnp.float32)
    same_column = lax.rem(iota((2 * BS, BS), 0), QW) == lax.rem(iota((2 * BS, BS), 1), QW)
    same_set = iota((2 * BS, BS), 0) // BS == iota((2 * BS, BS), 1) // (2 * QW)

    def terms(start):
        part = jnp.dot(a2[pl.ds(start, half), :], w[...], preferred_element_type=jnp.float32)
        return 4.0 * part[:, :BS] - 3.0 * part[:, BS:]

    def finish(j):
        r_copy(j).wait_recv()
        summed = (own[j] + rs_recv[j]).astype(jnp.bfloat16)
        src, dst = iota((BS, NT * BS), 0), iota((BS, NT * BS), 1)
        put = one_hot((dst // BS == src // QW) & (lax.rem(dst, BS) == lax.rem(src, QW) + j * QW))
        moved = jnp.dot(summed, put, preferred_element_type=jnp.float32)
        if j == 0:
            total[...] = moved
        elif j < NCH - 1:
            total[...] += moved
        else:
            out_ref[...] = (total[...] + moved).astype(jnp.bfloat16)

    own_start = pl.multiple_of(layer * half, half)
    other_start = pl.multiple_of((1 - layer) * half, half)
    for j in range(NCH):
        mine = [p for p in range(n_p) if PIECES[p][0] == j]
        for q in (0, *reversed(z_order)):
            if q:
                for p in mine:
                    z_copy(p, q).wait_recv()
            if j == 0:
                n = PIECES[IDS][2]
                ids = z_recv[IDS][q, n : n + EXTRA].astype(jnp.float32)[0:1]
                pt[q] = one_hot((ids == target) & same_column & same_set)
            tiles = [z_recv[p][q, 0 : PIECES[p][2]] for p in mine]
            placed = lax.dot_general(
                tiles[0] if len(tiles) == 1 else jnp.concatenate(tiles, axis=0),
                pt[q],
                (((1,), (1,)), ((), ())),
                preferred_element_type=jnp.float32,
            )
            w[q * BS : (q + 1) * BS, :] = placed.astype(jnp.bfloat16)
        rs_send[j] = terms(other_start)
        r_copy(j).start()
        own[j] = terms(own_start)
        if j:
            finish(j - 1)
    finish(NCH - 1)

    for p in range(n_p):
        for d in y_order:
            y_copy(p, d).wait_send()
        for q in z_order:
            z_copy(p, q).wait_send()
    for j in range(NCH):
        r_copy(j).wait_send()


def body(slab_tiles, x_tiles, x_cols, x2_tiles, x2_cols, requests, out_cols):
    n_row, n_col = lax.axis_size("row"), lax.axis_size("col")
    bs, sr, _, n_req, _ = slab_tiles.shape
    n_out = out_cols.shape[2]
    rows = bs * sr
    half, n_p = rows // 2, len(PIECES)
    vmem = pl.BlockSpec(memory_space=pltpu.VMEM)
    anywhere = pl.BlockSpec(memory_space=pl.ANY)
    bf16, f32 = jnp.bfloat16, jnp.float32
    out = pl.pallas_call(
        functools.partial(kernel, (n_row, n_col, n_req)),
        name="purify",
        out_shape=jax.ShapeDtypeStruct((half, n_out * bs), bf16),
        in_specs=[anywhere] * 7,
        out_specs=vmem,
        scratch_shapes=[
            pltpu.SMEM((1, 2, n_col), jnp.int32),
            pltpu.SMEM((1, 2, n_col), jnp.int32),
            pltpu.SMEM((1, n_req, n_row), jnp.int32),
            pltpu.SMEM((1, 1, n_out), jnp.int32),
            pltpu.VMEM((2, n_col, 2, bs, bs), bf16),
            pltpu.VMEM((rows * n_req, bs), bf16),
            pltpu.VMEM((rows, n_req * bs), bf16),
            pltpu.VMEM((n_req, 2 * bs, bs), bf16),
            pltpu.VMEM((n_req * bs, 2 * bs), bf16),
            pltpu.VMEM((NCH, half, bs), f32),
            pltpu.VMEM((NCH, half, bs), f32),
            pltpu.VMEM((NCH, half, bs), f32),
        ]
        + [pltpu.VMEM((half, n_out * bs), f32)]
        + [pltpu.VMEM((n_col, piece_rows(p), bs), bf16) for p in range(n_p)] * 2
        + [pltpu.VMEM((n_req, piece_rows(p), bs), bf16) for p in range(n_p)] * 2
        + [
            pltpu.SemaphoreType.DMA((7,)),
            pltpu.SemaphoreType.DMA((n_p, n_col)),
            pltpu.SemaphoreType.DMA((n_p, n_col)),
            pltpu.SemaphoreType.DMA((n_p, n_req)),
            pltpu.SemaphoreType.DMA((n_p, n_req)),
            pltpu.SemaphoreType.DMA((NCH,)),
            pltpu.SemaphoreType.DMA((NCH,)),
            pltpu.SemaphoreType.REGULAR((n_col,)),
            pltpu.SemaphoreType.REGULAR((n_req,)),
        ],
        compiler_params=pltpu.CompilerParams(collective_id=0, has_side_effects=True),
    )(
        x_tiles.reshape(x_tiles.shape[1:]),
        x2_tiles.reshape(x2_tiles.shape[1:]),
        slab_tiles.reshape(rows * n_req, bs),
        jnp.swapaxes(x_cols, 1, 2),
        jnp.swapaxes(x2_cols, 1, 2),
        jnp.swapaxes(requests, 1, 2),
        out_cols,
    )
    return out.reshape(bs // 2, sr, 1, n_out, bs)


def solution(mesh):
    placed = (
        P(None, "row", "layer", None, None),
        P(("layer", "row", "col"), None, None, None, None),
        P(("layer", "row", "col"), None, None),
        P(("layer", "row", "col"), None, None, None, None),
        P(("layer", "row", "col"), None, None),
        P("layer", None, None),
        P("row", "col", None),
    )
    return jax.shard_map(
        body,
        mesh=mesh,
        in_specs=placed,
        out_specs=P("layer", "row", "col", None, None),
        check_vma=False,
    )
```

```python
import functools

import jax
import jax.numpy as jnp
from jax import lax
from jax.experimental import pallas as pl
from jax.experimental.pallas import tpu as pltpu
from jax.sharding import PartitionSpec as P

MESH = pl.DeviceIdType.MESH
BS = 128
NT = 4
CHUNKS = ((0, 1), (32, 1), (64, 1), (96, 1))
NCH = len(CHUNKS)
GROUPS = (1,)
PIECES = (
    (0, 0, 16), (0, 16, 32), (0, 48, 64), (0, 112, 16), (-1, 0, 1), (1, 0, 128), (2, 0, 128), (3, 0, 128),
)


def one_hot(cond):
    return jnp.where(cond, 1.0, 0.0).astype(jnp.bfloat16)


def iota(shape, dim):
    return lax.broadcasted_iota(jnp.int32, shape, dim)


IDS = 4
GATED = 6


def piece(p, count):
    j, _, n = PIECES[p]
    return pltpu.VMEM((count, n, BS), jnp.bfloat16 if j >= 0 else jnp.float32)


def kernel(
    sizes, x_hbm, x2_hbm, a_hbm, xc_hbm, x2c_hbm, req_hbm, oc_hbm, out_ref, xc, x2c, req, oc, xv,
    a_raw, a2, pt, w, put, total, *rest
):
    n_row, n_col, n_req = sizes
    n_p = len(PIECES)
    y_send, y_recv, z_send, z_recv = (rest[i * n_p : (i + 1) * n_p] for i in range(4))
    rest = rest[4 * n_p :]
    rs_send, rs_recv, own = (rest[i * NCH : (i + 1) * NCH] for i in range(3))
    load_sem, y_ss, y_rs, z_ss, z_rs, r_ss, r_rs, y_hello, z_hello = rest[3 * NCH :]
    layer, row, col = (lax.axis_index(a) for a in ("layer", "row", "col"))
    stride = n_row // n_col
    place = row // stride
    half = total.shape[0]

    loads = [
        pltpu.make_async_copy(x_hbm, xv.at[0], load_sem.at[0]),
        pltpu.make_async_copy(x2_hbm, xv.at[1], load_sem.at[1]),
        pltpu.make_async_copy(a_hbm, a_raw, load_sem.at[2]),
        pltpu.make_async_copy(req_hbm, req, load_sem.at[3]),
        pltpu.make_async_copy(xc_hbm, xc, load_sem.at[4]),
        pltpu.make_async_copy(x2c_hbm, x2c, load_sem.at[5]),
        pltpu.make_async_copy(oc_hbm, oc, load_sem.at[6]),
    ]
    def y_device(d):
        return (layer, row, lax.rem(col + d, n_col))

    def z_device(q):
        return (layer, lax.rem(row - stride * q + n_row, n_row), col)

    def y_lower(d):
        return col + d >= n_col

    def z_lower(q):
        return q <= place

    barrier = pltpu.get_barrier_semaphore()

    def signal(sem, device):
        pl.semaphore_signal(sem, inc=1, device_id=device, device_id_type=MESH)

    signal(barrier, (1 - layer, row, col))
    for d in range(1, n_col):
        pl.when(jnp.logical_not(y_lower(d)))(functools.partial(signal, barrier, y_device(d)))
    for q in range(1, n_req):
        pl.when(jnp.logical_not(z_lower(q)))(functools.partial(signal, barrier, z_device(q)))

    for load in loads:
        load.start()

    pl.semaphore_wait(barrier, 1 + col + place)
    for q in range(1, n_req):
        pl.when(z_lower(q))(functools.partial(signal, z_hello.at[n_req - q], z_device(q)))
    for d in range(1, n_col):
        pl.when(y_lower(d))(functools.partial(signal, y_hello.at[n_col - d], y_device(d)))

    def y_copy(p, d):
        return pltpu.make_async_remote_copy(
            src_ref=y_send[p].at[lax.rem(col + d, n_col)],
            dst_ref=y_recv[p].at[col],
            send_sem=y_ss.at[p, d],
            recv_sem=y_rs.at[p, d],
            device_id=y_device(d),
            device_id_type=MESH,
        )

    def z_copy(p, q):
        return pltpu.make_async_remote_copy(
            src_ref=z_send[p].at[q],
            dst_ref=z_recv[p].at[q],
            send_sem=z_ss.at[p, q],
            recv_sem=z_rs.at[p, q],
            device_id=z_device(q),
            device_id_type=MESH,
        )

    def r_copy(j):
        return pltpu.make_async_remote_copy(
            src_ref=rs_send[j],
            dst_ref=rs_recv[j],
            send_sem=r_ss.at[j],
            recv_sem=r_rs.at[j],
            device_id=(1 - layer, row, col),
            device_id_type=MESH,
        )

    y_order = sorted(range(1, n_col), key=lambda d: abs(2 * d - n_col))
    z_order = sorted(range(1, n_req), key=lambda q: abs(2 * q - n_req))

    def heard(sem, *copies):
        pl.semaphore_wait(sem, 1)
        for copy in copies:
            copy.start()

    def build(p):
        j, at, n = PIECES[p]
        start, groups = CHUNKS[j]
        wide = BS // groups
        src, dst = iota((NT * BS, BS), 0), iota((NT * BS, BS), 1)
        within = lax.rem(dst, wide)
        width = wide // NT
        keep = (src // BS == within // width) & (
            lax.rem(src, BS) == lax.rem(within, width) + start
        )
        step = n_col if n <= 32 else 1
        for c in range(0, n_col, step):
            chunk = None
            for g in range(groups):
                rows = pl.ds(at + g * (BS // groups), n)
                tiles = [
                    xv[i, c : c + step, u, rows].reshape(step * n, BS)
                    for i in range(2)
                    for u in range(2)
                ]
                take = one_hot(keep & (dst // wide == g))
                part = jnp.dot(
                    jnp.concatenate(tiles, axis=1), take, preferred_element_type=jnp.float32
                )
                chunk = part if chunk is None else chunk + part
            y_send[p][c : c + step, 0:n] = chunk.astype(jnp.bfloat16).reshape(step, n, BS)

    def build_ids():
        slot = iota((1, BS), 1) // (BS // NT)
        for c in range(n_col):
            first = jnp.where(slot < 1, xc[0, 0, c], xc[0, 1, c])
            second = jnp.where(slot < 3, x2c[0, 0, c], x2c[0, 1, c])
            y_send[IDS][c] = jnp.where(slot < 2, first, second).astype(jnp.float32)

    def send(p):
        for d in y_order:
            if p == 0:
                pl.when(y_lower(d))(y_copy(p, d).start)
            else:
                y_copy(p, d).start()
        if p == 0:
            for d in range(1, n_col):
                wait = functools.partial(heard, y_hello.at[d], y_copy(p, d))
                pl.when(jnp.logical_not(y_lower(d)))(wait)
        y_recv[p][col] = y_send[p][col]

    def forward(p):
        for d in y_order:
            y_copy(p, d).wait_recv()
        for q in z_order:
            z_send[p][q] = y_recv[p][owners[q]]
            if p < GATED:
                pl.when(z_lower(q))(z_copy(p, q).start)
            else:
                z_copy(p, q).start()
        z_recv[p][0] = y_recv[p][owners[0]]

    def upper(pieces, steps, wait):
        for k in steps:
            q = n_req - k
            copies = [z_copy(p, q) for p in pieces]

            def go(q=q, copies=copies):
                if wait:
                    heard(z_hello.at[q], *copies)
                else:
                    for copy in copies:
                        copy.start()

            pl.when(jnp.logical_not(z_lower(q)))(go)

    loads[0].wait()
    loads[1].wait()
    build(0)
    send(0)
    build(1)
    send(1)
    build(2)
    send(2)
    for load in loads[3:]:
        load.wait()
    owners = []
    for q in range(n_req):
        reader = lax.rem(row - stride * q + n_row, n_row)
        owners.append(lax.rem(req[0, q, reader], n_col))

    build(3)
    send(3)
    build_ids()
    send(IDS)
    build(5)
    send(5)

    group = BS // n_req
    to_row, from_row = iota((BS, BS), 0), iota((BS, BS), 1)
    swap = one_hot(
        (to_row // group == lax.rem(from_row, n_req)) & (lax.rem(to_row, group) == from_row // n_req)
    )

    def regroup(i, carry):
        block = a_raw[pl.ds(pl.multiple_of(i * BS, BS), BS), :]
        moved = jnp.dot(swap, block, preferred_element_type=jnp.float32).astype(jnp.bfloat16)
        for q in range(n_req):
            a2[pl.ds(pl.multiple_of(i * group, group), group), q * BS : (q + 1) * BS] = moved[
                q * group : (q + 1) * group
            ]
        return carry

    near, middle, far = (1, 2), (3, 4), range(5, n_req)
    forward(0)
    upper((0,), near, True)
    forward(1)
    upper((1,), near, False)
    forward(2)
    upper((2,), near, False)
    upper((0, 1, 2), middle, True)
    forward(3)
    upper((3,), (*near, *middle), False)
    build(6)
    send(6)
    forward(4)
    upper((4,), (*near, *middle), False)
    forward(5)
    upper((5,), (*near, *middle), False)
    upper(range(GATED), far, True)
    for p in range(7, n_p):
        build(p)
        send(p)
    loads[2].wait()
    lax.fori_loop(0, a_raw.shape[0] // BS, regroup, 0, unroll=4)

    def first_put(j):
        return sum(groups for _, groups in CHUNKS[:j])

    for j, (start, groups) in enumerate(CHUNKS):
        wide = BS // groups
        width = wide // NT
        src, dst = iota((BS, NT * BS), 0), iota((BS, NT * BS), 1)
        within = lax.rem(src, wide)
        keep = (dst // BS == within // width) & (
            lax.rem(dst, BS) == lax.rem(within, width) + start
        )
        for g in range(groups):
            put[first_put(j) + g] = one_hot(keep & (src // wide == g))

    for p in range(GATED, n_p):
        forward(p)

    def placing(groups, ids, g):
        wide = BS // groups
        width = wide // NT
        n = max(2 * wide, BS)
        to, at = iota((n, BS), 0), iota((n, BS), 1)
        block = lax.rem(to, wide) // width
        target = jnp.where(
            block < 2,
            jnp.where(block < 1, oc[0, 0, 0], oc[0, 0, 1]),
            jnp.where(block < 3, oc[0, 0, 2], oc[0, 0, 3]),
        )
        target = target.astype(jnp.float32)
        same_column = lax.rem(to, width) == lax.rem(at, width)
        same_set = to // wide == lax.rem(at, wide) // (2 * width)
        return one_hot((ids == target) & same_column & same_set & (at // wide == g))

    def terms(j, start):
        groups = CHUNKS[j][1]
        wide = BS // groups
        n = max(2 * wide, BS)
        part = jnp.dot(
            a2[pl.ds(start, half), :], w[:, 0:n], preferred_element_type=jnp.float32
        )
        if groups == 1:
            return 4.0 * part[:, :BS] - 3.0 * part[:, BS:]
        part = 4.0 * part - 3.0 * pltpu.roll(part, BS - wide, 1)
        rows = half // groups
        packed = part[0:rows]
        lane = iota((rows, BS), 1)
        for g in range(1, groups):
            moved = pltpu.roll(part[g * rows : (g + 1) * rows], g * wide, 1)
            packed = jnp.where(lane // wide == g, moved, packed)
        return packed

    def finish(j):
        groups = CHUNKS[j][1]
        rows = half // groups
        r_copy(j).wait_recv()
        summed = (own[j][...] + rs_recv[j][...]).astype(jnp.bfloat16)
        for g in range(groups):
            moved = jnp.dot(summed, put[first_put(j) + g], preferred_element_type=jnp.float32)
            at = slice(g * rows, (g + 1) * rows)
            if j == 0:
                total[at] = moved
            elif j < NCH - 1:
                total[at] += moved
            else:
                out_ref[at] = (total[at] + moved).astype(jnp.bfloat16)

    own_start = pl.multiple_of(layer * half, half)
    other_start = pl.multiple_of((1 - layer) * half, half)
    for j in range(NCH):
        groups = CHUNKS[j][1]
        n = max(2 * BS // groups, BS)
        depth = BS // groups
        mine = [p for p in range(n_p) if PIECES[p][0] == j]
        kinds = sum(GROUPS[: GROUPS.index(groups)])
        for q in (0, *z_order):
            if q:
                for p in mine:
                    z_copy(p, q).wait_recv()
            if j == 0:
                if q:
                    z_copy(IDS, q).wait_recv()
                pt[0, q] = placing(groups, z_recv[IDS][q], 0)
            tiles = [z_recv[p][q, 0 : PIECES[p][2]] for p in mine]
            tile = tiles[0] if len(tiles) == 1 else jnp.concatenate(tiles, axis=0)
            for g in range(groups):
                placed = lax.dot_general(
                    tile,
                    pt[kinds + g, q, 0:n],
                    (((1,), (1,)), ((), ())),
                    preferred_element_type=jnp.float32,
                )
                at = q * BS + g * depth
                w[at : at + depth, 0:n] = placed.astype(jnp.bfloat16)
        rs_send[j][...] = terms(j, other_start)
        r_copy(j).start()
        own[j][...] = terms(j, own_start)
        if j:
            finish(j - 1)
    finish(NCH - 1)

    for p in range(n_p):
        for d in y_order:
            y_copy(p, d).wait_send()
        for q in z_order:
            z_copy(p, q).wait_send()
    for j in range(NCH):
        r_copy(j).wait_send()


def body(slab_tiles, x_tiles, x_cols, x2_tiles, x2_cols, requests, out_cols):
    n_row, n_col = lax.axis_size("row"), lax.axis_size("col")
    bs, sr, _, n_req, _ = slab_tiles.shape
    n_out = out_cols.shape[2]
    rows = bs * sr
    half, n_p = rows // 2, len(PIECES)
    vmem = pl.BlockSpec(memory_space=pltpu.VMEM)
    anywhere = pl.BlockSpec(memory_space=pl.ANY)
    bf16, f32 = jnp.bfloat16, jnp.float32
    out = pl.pallas_call(
        functools.partial(kernel, (n_row, n_col, n_req)),
        name="purify",
        out_shape=jax.ShapeDtypeStruct((half, n_out * bs), bf16),
        in_specs=[anywhere] * 7,
        out_specs=vmem,
        scratch_shapes=[
            pltpu.SMEM((1, 2, n_col), jnp.int32),
            pltpu.SMEM((1, 2, n_col), jnp.int32),
            pltpu.SMEM((1, n_req, n_row), jnp.int32),
            pltpu.SMEM((1, 1, n_out), jnp.int32),
            pltpu.VMEM((2, n_col, 2, bs, bs), bf16),
            pltpu.VMEM((rows * n_req, bs), bf16),
            pltpu.VMEM((rows, n_req * bs), bf16),
            pltpu.VMEM((sum(GROUPS), n_req, 2 * bs, bs), bf16),
            pltpu.VMEM((n_req * bs, 2 * bs), bf16),
            pltpu.VMEM((sum(g for _, g in CHUNKS), bs, NT * bs), bf16),
            pltpu.VMEM((half, n_out * bs), f32),
        ]
        + [piece(p, n_col) for p in range(n_p)] * 2
        + [piece(p, n_req) for p in range(n_p)] * 2
        + [pltpu.VMEM((half // g, bs), f32) for _, g in CHUNKS] * 3
        + [
            pltpu.SemaphoreType.DMA((7,)),
            pltpu.SemaphoreType.DMA((n_p, n_col)),
            pltpu.SemaphoreType.DMA((n_p, n_col)),
            pltpu.SemaphoreType.DMA((n_p, n_req)),
            pltpu.SemaphoreType.DMA((n_p, n_req)),
            pltpu.SemaphoreType.DMA((NCH,)),
            pltpu.SemaphoreType.DMA((NCH,)),
            pltpu.SemaphoreType.REGULAR((n_col,)),
            pltpu.SemaphoreType.REGULAR((n_req,)),
        ],
        compiler_params=pltpu.CompilerParams(collective_id=0, has_side_effects=True),
    )(
        x_tiles.reshape(x_tiles.shape[1:]),
        x2_tiles.reshape(x2_tiles.shape[1:]),
        slab_tiles.reshape(rows * n_req, bs),
        jnp.swapaxes(x_cols, 1, 2),
        jnp.swapaxes(x2_cols, 1, 2),
        jnp.swapaxes(requests, 1, 2),
        out_cols,
    )
    return out.reshape(bs // 2, sr, 1, n_out, bs)


def solution(mesh):
    placed = (
        P(None, "row", "layer", None, None),
        P(("layer", "row", "col"), None, None, None, None),
        P(("layer", "row", "col"), None, None),
        P(("layer", "row", "col"), None, None, None, None),
        P(("layer", "row", "col"), None, None),
        P("layer", None, None),
        P("row", "col", None),
    )
    return jax.shard_map(
        body,
        mesh=mesh,
        in_specs=placed,
        out_specs=P("layer", "row", "col", None, None),
        check_vma=False,
    )
```

```python
import functools

import jax
import jax.numpy as jnp
from jax import lax
from jax.experimental import pallas as pl
from jax.experimental.pallas import tpu as pltpu
from jax.sharding import PartitionSpec as P

MESH = pl.DeviceIdType.MESH
BS = 128
NT = 4
CHUNKS = ((0, 1), (32, 1), (64, 1), (96, 1))
NCH = len(CHUNKS)
GROUPS = (1,)
PIECES = (
    (0, 0, 32), (0, 32, 64), (0, 96, 32), (-1, 0, 1), (1, 0, 128), (2, 0, 128), (3, 0, 128),
)


def one_hot(cond):
    return jnp.where(cond, 1.0, 0.0).astype(jnp.bfloat16)


def iota(shape, dim):
    return lax.broadcasted_iota(jnp.int32, shape, dim)


IDS = 3
GATED = 5


def piece(p, count):
    j, _, n = PIECES[p]
    return pltpu.VMEM((count, n, BS), jnp.bfloat16 if j >= 0 else jnp.float32)


def kernel(
    sizes, x_hbm, x2_hbm, a_hbm, xc_hbm, x2c_hbm, req_hbm, oc_hbm, out_ref, xc, x2c, req, oc, xv,
    a_raw, a2, pt, w, put, total, *rest
):
    n_row, n_col, n_req = sizes
    n_p = len(PIECES)
    y_send, y_recv, z_send, z_recv = (rest[i * n_p : (i + 1) * n_p] for i in range(4))
    rest = rest[4 * n_p :]
    rs_send, rs_recv, own = (rest[i * NCH : (i + 1) * NCH] for i in range(3))
    load_sem, y_ss, y_rs, z_ss, z_rs, r_ss, r_rs, y_hello, z_hello = rest[3 * NCH :]
    layer, row, col = (lax.axis_index(a) for a in ("layer", "row", "col"))
    stride = n_row // n_col
    place = row // stride
    half = total.shape[0]

    loads = [
        pltpu.make_async_copy(x_hbm, xv.at[0], load_sem.at[0]),
        pltpu.make_async_copy(x2_hbm, xv.at[1], load_sem.at[1]),
        pltpu.make_async_copy(a_hbm, a_raw, load_sem.at[2]),
        pltpu.make_async_copy(req_hbm, req, load_sem.at[3]),
        pltpu.make_async_copy(xc_hbm, xc, load_sem.at[4]),
        pltpu.make_async_copy(x2c_hbm, x2c, load_sem.at[5]),
        pltpu.make_async_copy(oc_hbm, oc, load_sem.at[6]),
    ]
    def y_device(d):
        return (layer, row, lax.rem(col + d, n_col))

    def z_device(q):
        return (layer, lax.rem(row - stride * q + n_row, n_row), col)

    def y_lower(d):
        return col + d >= n_col

    def z_lower(q):
        return q <= place

    barrier = pltpu.get_barrier_semaphore()

    def signal(sem, device):
        pl.semaphore_signal(sem, inc=1, device_id=device, device_id_type=MESH)

    signal(barrier, (1 - layer, row, col))
    for d in range(1, n_col):
        pl.when(jnp.logical_not(y_lower(d)))(functools.partial(signal, barrier, y_device(d)))
    for q in range(1, n_req):
        pl.when(jnp.logical_not(z_lower(q)))(functools.partial(signal, barrier, z_device(q)))

    for load in loads:
        load.start()

    pl.semaphore_wait(barrier, 1 + col + place)
    for q in range(1, n_req):
        pl.when(z_lower(q))(functools.partial(signal, z_hello.at[n_req - q], z_device(q)))
    for d in range(1, n_col):
        pl.when(y_lower(d))(functools.partial(signal, y_hello.at[n_col - d], y_device(d)))

    def y_copy(p, d):
        return pltpu.make_async_remote_copy(
            src_ref=y_send[p].at[lax.rem(col + d, n_col)],
            dst_ref=y_recv[p].at[col],
            send_sem=y_ss.at[p, d],
            recv_sem=y_rs.at[p, d],
            device_id=y_device(d),
            device_id_type=MESH,
        )

    def z_copy(p, q):
        return pltpu.make_async_remote_copy(
            src_ref=z_send[p].at[q],
            dst_ref=z_recv[p].at[q],
            send_sem=z_ss.at[p, q],
            recv_sem=z_rs.at[p, q],
            device_id=z_device(q),
            device_id_type=MESH,
        )

    def r_copy(j):
        return pltpu.make_async_remote_copy(
            src_ref=rs_send[j],
            dst_ref=rs_recv[j],
            send_sem=r_ss.at[j],
            recv_sem=r_rs.at[j],
            device_id=(1 - layer, row, col),
            device_id_type=MESH,
        )

    y_order = sorted(range(1, n_col), key=lambda d: abs(2 * d - n_col))
    z_order = sorted(range(1, n_req), key=lambda q: abs(2 * q - n_req))

    def heard(sem, *copies):
        pl.semaphore_wait(sem, 1)
        for copy in copies:
            copy.start()

    def build(p):
        j, at, n = PIECES[p]
        start, groups = CHUNKS[j]
        wide = BS // groups
        src, dst = iota((NT * BS, BS), 0), iota((NT * BS, BS), 1)
        within = lax.rem(dst, wide)
        width = wide // NT
        keep = (src // BS == within // width) & (
            lax.rem(src, BS) == lax.rem(within, width) + start
        )
        step = n_col if n <= 32 else 1
        for c in range(0, n_col, step):
            chunk = None
            for g in range(groups):
                rows = pl.ds(at + g * (BS // groups), n)
                tiles = [
                    xv[i, c : c + step, u, rows].reshape(step * n, BS)
                    for i in range(2)
                    for u in range(2)
                ]
                take = one_hot(keep & (dst // wide == g))
                part = jnp.dot(
                    jnp.concatenate(tiles, axis=1), take, preferred_element_type=jnp.float32
                )
                chunk = part if chunk is None else chunk + part
            y_send[p][c : c + step, 0:n] = chunk.astype(jnp.bfloat16).reshape(step, n, BS)

    def build_ids():
        slot = iota((1, BS), 1) // (BS // NT)
        for c in range(n_col):
            first = jnp.where(slot < 1, xc[0, 0, c], xc[0, 1, c])
            second = jnp.where(slot < 3, x2c[0, 0, c], x2c[0, 1, c])
            y_send[IDS][c] = jnp.where(slot < 2, first, second).astype(jnp.float32)

    def send(p):
        for d in y_order:
            if p == 0:
                pl.when(y_lower(d))(y_copy(p, d).start)
            else:
                y_copy(p, d).start()
        if p == 0:
            for d in range(1, n_col):
                wait = functools.partial(heard, y_hello.at[d], y_copy(p, d))
                pl.when(jnp.logical_not(y_lower(d)))(wait)
        y_recv[p][col] = y_send[p][col]

    def forward(p):
        for d in y_order:
            y_copy(p, d).wait_recv()
        for q in z_order:
            z_send[p][q] = y_recv[p][owners[q]]
            if p < GATED:
                pl.when(z_lower(q))(z_copy(p, q).start)
            else:
                z_copy(p, q).start()
        z_recv[p][0] = y_recv[p][owners[0]]

    def upper(pieces, steps, wait):
        for k in steps:
            q = n_req - k
            copies = [z_copy(p, q) for p in pieces]

            def go(q=q, copies=copies):
                if wait:
                    heard(z_hello.at[q], *copies)
                else:
                    for copy in copies:
                        copy.start()

            pl.when(jnp.logical_not(z_lower(q)))(go)

    loads[0].wait()
    loads[1].wait()
    build(0)
    send(0)
    build(1)
    send(1)
    build(2)
    send(2)
    for load in loads[3:]:
        load.wait()
    owners = []
    for q in range(n_req):
        reader = lax.rem(row - stride * q + n_row, n_row)
        owners.append(lax.rem(req[0, q, reader], n_col))

    build_ids()
    send(IDS)
    build(4)
    send(4)

    group = BS // n_req
    to_row, from_row = iota((BS, BS), 0), iota((BS, BS), 1)
    swap = one_hot(
        (to_row // group == lax.rem(from_row, n_req)) & (lax.rem(to_row, group) == from_row // n_req)
    )

    def regroup(i, carry):
        block = a_raw[pl.ds(pl.multiple_of(i * BS, BS), BS), :]
        moved = jnp.dot(swap, block, preferred_element_type=jnp.float32).astype(jnp.bfloat16)
        for q in range(n_req):
            a2[pl.ds(pl.multiple_of(i * group, group), group), q * BS : (q + 1) * BS] = moved[
                q * group : (q + 1) * group
            ]
        return carry

    near, middle, far = (1, 2), (3, 4), range(5, n_req)
    forward(0)
    upper((0,), near, True)
    forward(1)
    upper((1,), near, False)
    forward(2)
    upper((2,), near, False)
    upper((0, 1, 2), middle, True)
    forward(3)
    upper((3,), (*near, *middle), False)
    build(5)
    send(5)
    forward(4)
    upper((4,), (*near, *middle), False)
    upper(range(GATED), far, True)
    for p in range(6, n_p):
        build(p)
        send(p)
    loads[2].wait()
    lax.fori_loop(0, a_raw.shape[0] // BS, regroup, 0, unroll=4)

    def first_put(j):
        return sum(groups for _, groups in CHUNKS[:j])

    for j, (start, groups) in enumerate(CHUNKS):
        wide = BS // groups
        width = wide // NT
        src, dst = iota((BS, NT * BS), 0), iota((BS, NT * BS), 1)
        within = lax.rem(src, wide)
        keep = (dst // BS == within // width) & (
            lax.rem(dst, BS) == lax.rem(within, width) + start
        )
        for g in range(groups):
            put[first_put(j) + g] = one_hot(keep & (src // wide == g))

    for p in range(GATED, n_p):
        forward(p)

    def placing(groups, ids, g):
        wide = BS // groups
        width = wide // NT
        n = max(2 * wide, BS)
        to, at = iota((n, BS), 0), iota((n, BS), 1)
        block = lax.rem(to, wide) // width
        target = jnp.where(
            block < 2,
            jnp.where(block < 1, oc[0, 0, 0], oc[0, 0, 1]),
            jnp.where(block < 3, oc[0, 0, 2], oc[0, 0, 3]),
        )
        target = target.astype(jnp.float32)
        same_column = lax.rem(to, width) == lax.rem(at, width)
        same_set = to // wide == lax.rem(at, wide) // (2 * width)
        return one_hot((ids == target) & same_column & same_set & (at // wide == g))

    def terms(j, start):
        groups = CHUNKS[j][1]
        wide = BS // groups
        n = max(2 * wide, BS)
        part = jnp.dot(
            a2[pl.ds(start, half), :], w[:, 0:n], preferred_element_type=jnp.float32
        )
        if groups == 1:
            return 4.0 * part[:, :BS] - 3.0 * part[:, BS:]
        part = 4.0 * part - 3.0 * pltpu.roll(part, BS - wide, 1)
        rows = half // groups
        packed = part[0:rows]
        lane = iota((rows, BS), 1)
        for g in range(1, groups):
            moved = pltpu.roll(part[g * rows : (g + 1) * rows], g * wide, 1)
            packed = jnp.where(lane // wide == g, moved, packed)
        return packed

    def finish(j):
        groups = CHUNKS[j][1]
        rows = half // groups
        r_copy(j).wait_recv()
        summed = (own[j][...] + rs_recv[j][...]).astype(jnp.bfloat16)
        for g in range(groups):
            moved = jnp.dot(summed, put[first_put(j) + g], preferred_element_type=jnp.float32)
            at = slice(g * rows, (g + 1) * rows)
            if j == 0:
                total[at] = moved
            elif j < NCH - 1:
                total[at] += moved
            else:
                out_ref[at] = (total[at] + moved).astype(jnp.bfloat16)

    own_start = pl.multiple_of(layer * half, half)
    other_start = pl.multiple_of((1 - layer) * half, half)
    for j in range(NCH):
        groups = CHUNKS[j][1]
        n = max(2 * BS // groups, BS)
        depth = BS // groups
        mine = [p for p in range(n_p) if PIECES[p][0] == j]
        kinds = sum(GROUPS[: GROUPS.index(groups)])
        for q in (0, *z_order):
            if q:
                for p in mine:
                    z_copy(p, q).wait_recv()
            if j == 0:
                if q:
                    z_copy(IDS, q).wait_recv()
                pt[0, q] = placing(groups, z_recv[IDS][q], 0)
            tiles = [z_recv[p][q, 0 : PIECES[p][2]] for p in mine]
            tile = tiles[0] if len(tiles) == 1 else jnp.concatenate(tiles, axis=0)
            for g in range(groups):
                placed = lax.dot_general(
                    tile,
                    pt[kinds + g, q, 0:n],
                    (((1,), (1,)), ((), ())),
                    preferred_element_type=jnp.float32,
                )
                at = q * BS + g * depth
                w[at : at + depth, 0:n] = placed.astype(jnp.bfloat16)
        rs_send[j][...] = terms(j, other_start)
        r_copy(j).start()
        own[j][...] = terms(j, own_start)
        if j:
            finish(j - 1)
    finish(NCH - 1)

    for p in range(n_p):
        for d in y_order:
            y_copy(p, d).wait_send()
        for q in z_order:
            z_copy(p, q).wait_send()
    for j in range(NCH):
        r_copy(j).wait_send()


def body(slab_tiles, x_tiles, x_cols, x2_tiles, x2_cols, requests, out_cols):
    n_row, n_col = lax.axis_size("row"), lax.axis_size("col")
    bs, sr, _, n_req, _ = slab_tiles.shape
    n_out = out_cols.shape[2]
    rows = bs * sr
    half, n_p = rows // 2, len(PIECES)
    vmem = pl.BlockSpec(memory_space=pltpu.VMEM)
    anywhere = pl.BlockSpec(memory_space=pl.ANY)
    bf16, f32 = jnp.bfloat16, jnp.float32
    out = pl.pallas_call(
        functools.partial(kernel, (n_row, n_col, n_req)),
        name="purify",
        out_shape=jax.ShapeDtypeStruct((half, n_out * bs), bf16),
        in_specs=[anywhere] * 7,
        out_specs=vmem,
        scratch_shapes=[
            pltpu.SMEM((1, 2, n_col), jnp.int32),
            pltpu.SMEM((1, 2, n_col), jnp.int32),
            pltpu.SMEM((1, n_req, n_row), jnp.int32),
            pltpu.SMEM((1, 1, n_out), jnp.int32),
            pltpu.VMEM((2, n_col, 2, bs, bs), bf16),
            pltpu.VMEM((rows * n_req, bs), bf16),
            pltpu.VMEM((rows, n_req * bs), bf16),
            pltpu.VMEM((sum(GROUPS), n_req, 2 * bs, bs), bf16),
            pltpu.VMEM((n_req * bs, 2 * bs), bf16),
            pltpu.VMEM((sum(g for _, g in CHUNKS), bs, NT * bs), bf16),
            pltpu.VMEM((half, n_out * bs), f32),
        ]
        + [piece(p, n_col) for p in range(n_p)] * 2
        + [piece(p, n_req) for p in range(n_p)] * 2
        + [pltpu.VMEM((half // g, bs), f32) for _, g in CHUNKS] * 3
        + [
            pltpu.SemaphoreType.DMA((7,)),
            pltpu.SemaphoreType.DMA((n_p, n_col)),
            pltpu.SemaphoreType.DMA((n_p, n_col)),
            pltpu.SemaphoreType.DMA((n_p, n_req)),
            pltpu.SemaphoreType.DMA((n_p, n_req)),
            pltpu.SemaphoreType.DMA((NCH,)),
            pltpu.SemaphoreType.DMA((NCH,)),
            pltpu.SemaphoreType.REGULAR((n_col,)),
            pltpu.SemaphoreType.REGULAR((n_req,)),
        ],
        compiler_params=pltpu.CompilerParams(collective_id=0, has_side_effects=True),
    )(
        x_tiles.reshape(x_tiles.shape[1:]),
        x2_tiles.reshape(x2_tiles.shape[1:]),
        slab_tiles.reshape(rows * n_req, bs),
        jnp.swapaxes(x_cols, 1, 2),
        jnp.swapaxes(x2_cols, 1, 2),
        jnp.swapaxes(requests, 1, 2),
        out_cols,
    )
    return out.reshape(bs // 2, sr, 1, n_out, bs)


def solution(mesh):
    placed = (
        P(None, "row", "layer", None, None),
        P(("layer", "row", "col"), None, None, None, None),
        P(("layer", "row", "col"), None, None),
        P(("layer", "row", "col"), None, None, None, None),
        P(("layer", "row", "col"), None, None),
        P("layer", None, None),
        P("row", "col", None),
    )
    return jax.shard_map(
        body,
        mesh=mesh,
        in_specs=placed,
        out_specs=P("layer", "row", "col", None, None),
        check_vma=False,
    )
```
